32 devices in a mesh: fsdp: 8 (over y, x, core), sp: 4 (over z).
Axes of the slice: x: 2, y: 2, z: 4, core: 2. Of those that a mesh axis runs over, the one named last changes fastest.
Arguments:
- tokens_in: bfloat16 [8, 1024, 1536], P('fsdp', 'sp')
- w_qkv: bfloat16 [1536, 3, 16, 128], P('fsdp', None, 'sp')
- grad_attn: bfloat16 [8, 1024, 16, 128], P('fsdp', None, 'sp'), may hold values from -6 to 6
- kv_tiles: int32 [16, 8, 4], P('sp'), may hold values from 0 to 7, as said below
- tile_live: int32 [16, 8, 4], P('sp'), may hold values from 0 to 1, as said below
Outputs:
- attention_out: bfloat16 [8, 1024, 16, 128], P('fsdp', None, 'sp')
- grad_tokens: bfloat16 [8, 1024, 1536], P('fsdp', 'sp')
The draws below stay inside these ranges and needn't reach their ends.
Inputs may be any that keep to these rules, and one draw needn't show every extreme that they name: `kv_tiles`: in every row the first slot names the query tile itself; the live tiles of one row are distinct. `tile_live`: the first slot of every row is live.
All inputs are finite; a program needn't handle non-finite values.
Results may differ from the reference program's by a relative error of at most 0.014.
The reference program's roundings to bfloat16 on the way (of `projected`, `probs_bf`, `grad_scores`, `grad_query`, `grad_key` and `grad_value`) count: a program that leaves them out, or rounds other values in their place, can miss the bound.
Values may be sent and summed in bfloat16 or wider, within the bound.
No kernel may reach another device: no remote copies, remote signals or barrier semaphores. Data moves between devices by JAX's collectives and lax.ppermute only.
A program may use at most 128 MiB of HBM per device.

```python
import jax
import jax.numpy as jnp
from jax import lax

D = 1536
HEADS = 16
HEAD = 128
TILE = 128
FRAME_TILES = 4
SEQS = 8
LENGTH = 1024
TILES = 8


def draw_tokens_in(key, part):
    inner = jax.random.fold_in(key, 21)
    base = jax.random.normal(inner, (SEQS, LENGTH, D), jnp.float32)
    return jnp.clip(base, -6.0, 6.0).astype(jnp.bfloat16)


def draw_w_qkv(key, part):
    inner = jax.random.fold_in(key, 31)
    factor = D ** (-0.5)
    base = jnp.clip(jax.random.normal(inner, (D, 3, HEADS, HEAD), jnp.float32), -4.0, 4.0)
    return (base * factor).astype(jnp.bfloat16)


def tile_layout(key):
    inner = jax.random.fold_in(key, 11)
    shape = (HEADS, TILES)
    tile_ids = jnp.arange(TILES, dtype=jnp.int32)[None, :] * jnp.ones(shape, jnp.int32)
    frame = tile_ids // FRAME_TILES
    spot = tile_ids % FRAME_TILES
    frames = TILES // FRAME_TILES
    turn = jax.random.randint(jax.random.fold_in(inner, 1), shape, 1, FRAME_TILES)
    same_frame = frame * FRAME_TILES + (spot + turn) % FRAME_TILES
    before_spot = jax.random.randint(jax.random.fold_in(inner, 2), shape, 0, FRAME_TILES)
    after_spot = jax.random.randint(jax.random.fold_in(inner, 3), shape, 0, FRAME_TILES)
    before = jnp.maximum(frame - 1, 0) * FRAME_TILES + before_spot
    after = jnp.minimum(frame + 1, frames - 1) * FRAME_TILES + after_spot
    listed = jnp.stack([tile_ids, same_frame, before, after], axis=-1).astype(jnp.int32)
    keep = jax.random.randint(jax.random.fold_in(inner, 4), (HEADS, TILES, 4), 0, 4) > 0
    always = jnp.ones(shape, dtype=bool)
    inside = jnp.stack([always, always, frame >= 1, frame + 1 < frames], axis=-1)
    first = jnp.arange(4, dtype=jnp.int32) == 0
    live = keep & inside | first
    return (listed, live.astype(jnp.int32))


def draw_kv_tiles(key, part):
    listed, live = tile_layout(key)
    return listed


def draw_tile_live(key, part):
    listed, live = tile_layout(key)
    return live


def steps_of(stream_key, shape, cuts, low, top_value):
    def one(position, blocks):
        heights = jax.random.uniform(jax.random.fold_in(jax.random.fold_in(stream_key, 6), position), (blocks,), jnp.float32, low / len(cuts), top_value / len(cuts))
        return jnp.repeat(jnp.exp(heights), shape[position] // blocks).reshape((-1,) + (1,) * (len(shape) - position - 1))

    gain = one(*cuts[0])
    for cut in cuts[1:]:
        gain = gain * one(*cut)
    return gain


def bell_draw(key, extent, width, reach, cuts=(), kind=jnp.bfloat16):
    drawn = jax.random.normal(key, extent, jnp.float32) * width
    if len(cuts) > 0:
        drawn = steps_of(key, extent, cuts, -0.22, 0.18) * drawn
    return jnp.clip(drawn, min=-reach, max=reach).astype(kind)


def setup_inputs(seed: int = 0) -> dict:
    splits = jax.random.split(jax.random.key(seed), 6)
    return {
        "tokens_in": draw_tokens_in(jax.random.fold_in(splits[5], 71), 0),
        "w_qkv": draw_w_qkv(jax.random.fold_in(splits[5], 71), 0),
        "grad_attn": bell_draw(splits[2], (SEQS, LENGTH, HEADS, HEAD), 1.0, 6.0, ((0, 8), (2, 4))),
        "kv_tiles": draw_kv_tiles(jax.random.fold_in(splits[5], 71), 0),
        "tile_live": draw_tile_live(jax.random.fold_in(splits[5], 71), 0),
    }


def tile_attention(head_qkv, grad_heads, kv_tiles, tile_live):
    length = head_qkv.shape[0]
    head_count = head_qkv.shape[2]
    channels = head_qkv.shape[3]
    tile_count = length // TILE
    slot_count = kv_tiles.shape[2]
    score_scale = HEAD ** -0.5

    def arrange(values):
        return jnp.transpose(values.reshape(tile_count, TILE, head_count, channels), (2, 0, 1, 3))

    def restore(values):
        return jnp.transpose(values, (1, 2, 0, 3)).reshape(length, head_count, channels)

    query_rows = arrange(head_qkv[:, 0]).astype(jnp.float32)
    key_all = arrange(head_qkv[:, 1]).astype(jnp.float32)
    value_all = arrange(head_qkv[:, 2]).astype(jnp.float32)
    grad_out = arrange(grad_heads).astype(jnp.float32)
    head_ids = jnp.arange(head_count, dtype=jnp.int32)[:, None, None]
    key_rows = key_all[head_ids, kv_tiles].reshape(head_count, tile_count, slot_count * TILE, channels)
    value_rows = value_all[head_ids, kv_tiles].reshape(head_count, tile_count, slot_count * TILE, channels)
    live_rows = jnp.repeat(tile_live > 0, TILE, axis=2)[:, :, None, :]
    scores = jnp.einsum("htqe,htke->htqk", query_rows, key_rows) * score_scale
    scores = jnp.where(live_rows, scores, -1e30)
    row_peak = jnp.max(scores, axis=3, keepdims=True)
    exp_scores = jnp.exp(scores - row_peak)
    probs_f = exp_scores / jnp.sum(exp_scores, axis=3, keepdims=True)
    probs_bf = probs_f.astype(jnp.bfloat16).astype(jnp.float32)
    attention_out = jnp.einsum("htqk,htke->htqe", probs_bf, value_rows).astype(jnp.bfloat16)
    grad_probs = jnp.einsum("htqe,htke->htqk", grad_out, value_rows)
    delta_sum = jnp.sum(probs_f * grad_probs, axis=3, keepdims=True)
    grad_scores = (probs_f * (grad_probs - delta_sum) * score_scale).astype(jnp.bfloat16).astype(jnp.float32)
    grad_query = jnp.einsum("htqk,htke->htqe", grad_scores, key_rows).astype(jnp.bfloat16)
    grad_key_rows = jnp.einsum("htqk,htqe->htke", grad_scores, query_rows)
    grad_value_rows = jnp.einsum("htqk,htqe->htke", probs_bf, grad_out)
    one_hot = (kv_tiles[..., None] == jnp.arange(tile_count, dtype=jnp.int32)).astype(jnp.float32)

    def collect(slot_rows):
        shaped = slot_rows.reshape(head_count, tile_count, slot_count, TILE, channels)
        return jnp.einsum("htsn,htsre->hnre", one_hot, shaped, precision=lax.Precision.HIGHEST)

    grad_key = collect(grad_key_rows).astype(jnp.bfloat16)
    grad_value = collect(grad_value_rows).astype(jnp.bfloat16)
    grad_qkv = jnp.stack([restore(grad_query), restore(grad_key), restore(grad_value)], axis=1)
    return restore(attention_out), grad_qkv


def reference(tokens_in, w_qkv, grad_attn, kv_tiles, tile_live):
    flat_weight = w_qkv.reshape(D, 3 * HEADS * HEAD)

    def one_sequence(pair):
        tokens, grad_heads = pair
        projected = jnp.dot(tokens, flat_weight, preferred_element_type=jnp.float32).astype(jnp.bfloat16)
        projected = projected.reshape(LENGTH, 3, HEADS, HEAD)
        attention_out, grad_qkv = tile_attention(projected, grad_heads, kv_tiles, tile_live)
        grad_tokens = jnp.dot(grad_qkv.reshape(LENGTH, 3 * HEADS * HEAD), flat_weight.T, preferred_element_type=jnp.float32)
        return attention_out, grad_tokens.astype(jnp.bfloat16)

    attention_out, grad_tokens = lax.map(one_sequence, (tokens_in, grad_attn))
    return attention_out, grad_tokens
```

```python
import functools

import jax
import jax.numpy as jnp
from jax import lax
from jax.experimental import pallas as pl
from jax.experimental.pallas import tpu as pltpu
from jax.sharding import PartitionSpec as P

HEAD = 128
TILE = 128
NN = (((1,), (0,)), ((), ()))
NT = (((1,), (1,)), ((), ()))


def dot(a, b, dims):
    return lax.dot_general(a, b, dims, preferred_element_type=jnp.float32)


def attention_kernel(
    place_ref, tiles_ref, live_ref, *refs, heads, slots, pieces
):
    piece_refs = refs[:pieces]
    dout_ref, out_ref, dqkv_ref, qkv_ref, kt_ref, vt_ref, dk_ref, dv_ref, sems = refs[pieces:]
    length = qkv_ref.shape[0]
    width = heads * HEAD
    tile_count = length // TILE
    scale = HEAD ** (-0.5)
    copies = []
    start = 0
    for number, piece in enumerate(piece_refs):
        size = piece.shape[0]
        copy = pltpu.make_async_copy(piece, qkv_ref.at[pl.ds(start, size)], sems.at[number])
        copy.start()
        copies.append(copy)
        start += size
    dk_ref[...] = jnp.zeros_like(dk_ref)
    dv_ref[...] = jnp.zeros_like(dv_ref)
    for copy in copies:
        copy.wait()
    for head in range(heads):
        at = head * HEAD
        kt_ref[head] = qkv_ref[:, width + at : width + at + HEAD].T
        vt_ref[head] = qkv_ref[:, 2 * width + at : 2 * width + at + HEAD].T

    def tile_rows(tile):
        return pl.ds(pl.multiple_of(tile * TILE, TILE), TILE)

    def one(head, tile):
        at = head * HEAD
        rows = tile_rows(tile)
        held = tile_rows(place_ref[tile])
        query = qkv_ref[held, at : at + HEAD]
        dout = dout_ref[rows, at : at + HEAD]
        base = (head * tile_count + tile) * slots
        spots = [tile_rows(place_ref[tiles_ref[base + s]]) for s in range(slots)]
        scores = []
        for s in range(slots):
            key = qkv_ref[spots[s], width + at : width + at + HEAD]
            part = dot(key, query, NT) * scale
            scores.append(jnp.where(live_ref[base + s] > 0, part, -1e30))
        peak = jnp.max(functools.reduce(jnp.maximum, scores), axis=0, keepdims=True)
        grown = [jnp.exp(part - peak) for part in scores]
        total = jnp.sum(functools.reduce(jnp.add, grown), axis=0, keepdims=True)
        inverse = 1.0 / total
        probs = [part * inverse for part in grown]
        probs_bf = jnp.concatenate([part.astype(jnp.bfloat16) for part in probs], axis=0)
        grads = []
        for s in range(slots):
            value = qkv_ref[spots[s], 2 * width + at : 2 * width + at + HEAD]
            grads.append(dot(value, dout, NT))
        delta = functools.reduce(jnp.add, [p * g for p, g in zip(probs, grads)])
        delta = jnp.sum(delta, axis=0, keepdims=True)
        dscores = jnp.concatenate(
            [(p * (g - delta) * scale).astype(jnp.bfloat16) for p, g in zip(probs, grads)], axis=0
        )
        value_t = jnp.concatenate([vt_ref[head, :, spot] for spot in spots], axis=1)
        key_t = jnp.concatenate([kt_ref[head, :, spot] for spot in spots], axis=1)
        out_ref[rows, at : at + HEAD] = dot(value_t, probs_bf, NN).T.astype(jnp.bfloat16)
        dqkv_ref[held, at : at + HEAD] = dot(key_t, dscores, NN).T.astype(jnp.bfloat16)
        dk = dot(dscores, query, NN)
        dv = dot(probs_bf, dout, NN)
        for s in range(slots):
            dk_ref[head, spots[s], :] += dk[s * TILE : (s + 1) * TILE]
            dv_ref[head, spots[s], :] += dv[s * TILE : (s + 1) * TILE]

    def step(tile, carry):
        for head in range(heads):
            one(head, tile)
        return carry

    lax.fori_loop(0, tile_count, step, 0)
    for head in range(heads):
        at = head * HEAD
        dqkv_ref[:, width + at : width + at + HEAD] = dk_ref[head].astype(jnp.bfloat16)
        dqkv_ref[:, 2 * width + at : 2 * width + at + HEAD] = dv_ref[head].astype(jnp.bfloat16)


def attention(pieces, dout, place, kv_tiles, tile_live):
    length = dout.shape[0]
    heads, tile_count, slots = kv_tiles.shape
    width = heads * HEAD
    smem = pl.BlockSpec(memory_space=pltpu.SMEM)
    vmem = pl.BlockSpec(memory_space=pltpu.VMEM)
    anywhere = pl.BlockSpec(memory_space=pl.ANY)
    return pl.pallas_call(
        functools.partial(attention_kernel, heads=heads, slots=slots, pieces=len(pieces)),
        out_shape=(
            jax.ShapeDtypeStruct((length, width), jnp.bfloat16),
            jax.ShapeDtypeStruct((length, 3 * width), jnp.bfloat16),
        ),
        in_specs=[smem, smem, smem] + [anywhere] * len(pieces) + [vmem],
        out_specs=(vmem, vmem),
        scratch_shapes=[
            pltpu.VMEM((length, 3 * width), jnp.bfloat16),
            pltpu.VMEM((heads, HEAD, length), jnp.bfloat16),
            pltpu.VMEM((heads, HEAD, length), jnp.bfloat16),
            pltpu.VMEM((heads, length, HEAD), jnp.float32),
            pltpu.VMEM((heads, length, HEAD), jnp.float32),
            pltpu.SemaphoreType.DMA((len(pieces),)),
        ],
        name="attention",
        cost_estimate=pl.CostEstimate(
            flops=12 * heads * tile_count * slots * TILE * TILE * HEAD,
            bytes_accessed=16 * length * width,
            transcendentals=heads * tile_count * slots * TILE * TILE,
        ),
        compiler_params=pltpu.CompilerParams(vmem_limit_bytes=48 << 20),
    )(place, kv_tiles.reshape(-1), tile_live.reshape(-1), *pieces, dout)


def folded(count):
    return list(range(0, count, 2)) + list(range(count - 1 - count % 2, 0, -2))


def gather_weights(w, axis, count):
    rows = w.shape[0]
    half = rows // 2
    mine = lax.axis_index(axis)

    def swap(value, bit):
        return lax.ppermute(value, axis, [(i, i ^ bit) for i in range(count)])

    held = {0: w}
    bits = [1 << b for b in range(1, count.bit_length() - 1)]
    if len(bits) == 2:
        low, high = bits
        held[low] = swap(w, low)
        held[high] = swap(w, high)
        held[low | high] = jnp.concatenate(
            [swap(held[high][:half], low), swap(held[low][half:], high)], axis=0
        )
    else:
        for bit in bits:
            held.update({k | bit: swap(v, bit) for k, v in list(held.items())})
    keys = list(held)
    other = swap(jnp.stack([held[k] for k in keys]), 1)
    whole = jnp.zeros((count * rows, w.shape[1]), w.dtype)
    for number, k in enumerate(keys):
        whole = lax.dynamic_update_slice(whole, held[k], ((mine ^ k) * rows, 0))
        whole = lax.dynamic_update_slice(whole, other[number], ((mine ^ k ^ 1) * rows, 0))
    return whole


def make_shards(fsdp_count, sp_count):
    order = folded(sp_count)
    ring = [(order[i], order[(i + 1) % sp_count]) for i in range(sp_count)]
    spot = [order.index(z) for z in range(sp_count)]
    arrived = [[(spot[z] - spot[c]) % sp_count for c in range(sp_count)] for z in range(sp_count)]

    def shards(tokens_in, w_qkv, grad_attn, kv_tiles, tile_live):
        tokens = tokens_in[0]
        chunk, depth = tokens.shape
        half = chunk // 2
        heads, tile_count, _ = kv_tiles.shape
        length = tile_count * TILE
        width = heads * HEAD
        w = gather_weights(w_qkv.reshape(w_qkv.shape[0], -1), "fsdp", fsdp_count)
        halves = [tokens[:half], tokens[half:]]
        parts = [tokens]
        for step in range(1, sp_count):
            halves = [lax.ppermute(part, "sp", ring) for part in halves]
            parts += halves
        pieces = [dot(part, w, NN).astype(jnp.bfloat16) for part in parts]
        per_chunk = chunk // TILE
        steps = jnp.array(arrived, jnp.int32)[lax.axis_index("sp")]
        tiles = jnp.arange(tile_count, dtype=jnp.int32)
        place = jnp.repeat(steps, per_chunk) * per_chunk + tiles % per_chunk
        out, dqkv = attention(pieces, grad_attn[0].reshape(length, width), place, kv_tiles, tile_live)

        def product(step, side):
            at = step * chunk + side * half
            return dot(dqkv[at : at + half], w, NT)

        arriving = [None, None]
        for step in range(1, sp_count + 1):
            for side in range(2):
                value = product(step % sp_count, side)
                if arriving[side] is not None:
                    value = value + arriving[side].astype(jnp.float32)
                value = value.astype(jnp.bfloat16)
                arriving[side] = lax.ppermute(value, "sp", ring) if step < sp_count else value
        grad_tokens = jnp.concatenate(arriving, axis=0)
        return out.reshape(1, length, heads, HEAD), grad_tokens[None]

    return shards


def solution(mesh):
    in_specs = (
        P("fsdp", "sp", None),
        P("fsdp", None, "sp", None),
        P("fsdp", None, "sp", None),
        P("sp", None, None),
        P("sp", None, None),
    )
    out_specs = (P("fsdp", None, "sp", None), P("fsdp", "sp", None))
    shards = make_shards(mesh.shape["fsdp"], mesh.shape["sp"])
    return jax.shard_map(shards, mesh=mesh, in_specs=in_specs, out_specs=out_specs, check_vma=False)
```

```python
import functools

import jax
import jax.numpy as jnp
from jax import lax
from jax.experimental import pallas as pl
from jax.experimental.pallas import tpu as pltpu
from jax.sharding import PartitionSpec as P


HEAD = 128
TILE = 128
NN = (((1,), (0,)), ((), ()))
NT = (((1,), (1,)), ((), ()))


def dot(a, b, dims):
    return lax.dot_general(a, b, dims, preferred_element_type=jnp.float32)


def project_kernel(owner_ref, *refs, shards, parts):
    shard_refs, part_refs = refs[:shards], refs[shards : shards + parts]
    w_ref, qkv_ref, tokens_ref, sems = refs[shards + parts :]
    rows = shard_refs[0].shape[0]
    copies = []
    for number, shard in enumerate(shard_refs):
        at = pl.ds(pl.multiple_of(owner_ref[number] * rows, rows), rows)
        copies.append(pltpu.make_async_copy(shard, w_ref.at[at], sems.at[number]))
    start = 0
    for number, part in enumerate(part_refs):
        at = pl.ds(start, part.shape[0])
        copies.append(pltpu.make_async_copy(part, tokens_ref.at[at], sems.at[shards + number]))
        start += part.shape[0]
    for copy in copies:
        copy.start()
    for copy in copies:
        copy.wait()

    def step(block, carry):
        at = pl.ds(pl.multiple_of(block * TILE, TILE), TILE)
        qkv_ref[at, :] = dot(tokens_ref[at, :], w_ref[...], NN).astype(jnp.bfloat16)
        return carry

    lax.fori_loop(0, start // TILE, step, 0)


def project(owners, shards, parts):
    _, width = shards[0].shape
    depth = parts[0].shape[1]
    length = sum(part.shape[0] for part in parts)
    anywhere = pl.BlockSpec(memory_space=pl.ANY)
    return pl.pallas_call(
        functools.partial(project_kernel, shards=len(shards), parts=len(parts)),
        out_shape=(
            jax.ShapeDtypeStruct((depth, width), jnp.bfloat16),
            jax.ShapeDtypeStruct((length, width), jnp.bfloat16),
        ),
        in_specs=[pl.BlockSpec(memory_space=pltpu.SMEM)] + [anywhere] * (len(shards) + len(parts)),
        out_specs=(pl.BlockSpec(memory_space=pltpu.VMEM),) * 2,
        scratch_shapes=[
            pltpu.VMEM((length, depth), jnp.bfloat16),
            pltpu.SemaphoreType.DMA((len(shards) + len(parts),)),
        ],
        name="project",
        cost_estimate=pl.CostEstimate(
            flops=2 * length * depth * width,
            bytes_accessed=4 * depth * width + 4 * length * width,
            transcendentals=0,
        ),
        compiler_params=pltpu.CompilerParams(vmem_limit_bytes=16 << 20),
    )(owners, *shards, *parts)


def product_kernel(dqkv_ref, w_ref, *out_refs, start):
    for out_ref in out_refs:
        rows = out_ref.shape[0]
        start = start % dqkv_ref.shape[0]
        out_ref[...] = dot(dqkv_ref[start : start + rows, :], w_ref[...], NT)
        start += rows


def products(dqkv, w, start, sizes):
    depth, width = w.shape
    return pl.pallas_call(
        functools.partial(product_kernel, start=start),
        out_shape=tuple(jax.ShapeDtypeStruct((size, depth), jnp.float32) for size in sizes),
        name="products",
        cost_estimate=pl.CostEstimate(
            flops=2 * sum(sizes) * depth * width,
            bytes_accessed=2 * depth * width + 6 * sum(sizes) * depth,
            transcendentals=0,
        ),
        compiler_params=pltpu.CompilerParams(vmem_limit_bytes=20 << 20),
    )(dqkv, w)


def finish_kernel(own_ref, low_ref, high_ref, out_ref):
    half = low_ref.shape[0]
    out_ref[:half, :] = (own_ref[:half, :] + low_ref[...].astype(jnp.float32)).astype(jnp.bfloat16)
    out_ref[half:, :] = (own_ref[half:, :] + high_ref[...].astype(jnp.float32)).astype(jnp.bfloat16)


def finish(own, low, high):
    return pl.pallas_call(
        finish_kernel,
        out_shape=jax.ShapeDtypeStruct(own.shape, jnp.bfloat16),
        name="finish",
        compiler_params=pltpu.CompilerParams(vmem_limit_bytes=8 << 20),
    )(own, low, high)


def attention_kernel(
    place_ref, tiles_ref, live_ref, early_ref, late_ref, last_ref, w_ref, dout_ref,
    out_ref, dqkv_ref, first_ref, second_ref, qkv_ref, kt_ref, vt_ref, dk_ref, dv_ref, sem,
    *, heads, slots, chunk,
):
    length = qkv_ref.shape[0]
    width = heads * HEAD
    tile_count = length // TILE
    scale = HEAD ** (-0.5)
    early = early_ref.shape[0]
    copy = pltpu.make_async_copy(early_ref, qkv_ref.at[pl.ds(0, early)], sem)
    copy.start()
    middle = early + late_ref.shape[0]
    qkv_ref[early:middle, :] = dot(late_ref[...], w_ref[...], NN).astype(jnp.bfloat16)
    qkv_ref[middle:, :] = dot(last_ref[...], w_ref[...], NN).astype(jnp.bfloat16)
    dk_ref[...] = jnp.zeros_like(dk_ref)
    dv_ref[...] = jnp.zeros_like(dv_ref)
    copy.wait()
    for head in range(heads):
        at = head * HEAD
        kt_ref[head] = qkv_ref[:, width + at : width + at + HEAD].T
        vt_ref[head] = qkv_ref[:, 2 * width + at : 2 * width + at + HEAD].T

    def tile_rows(tile):
        return pl.ds(pl.multiple_of(tile * TILE, TILE), TILE)

    def one(head, tile):
        at = head * HEAD
        rows = tile_rows(tile)
        held = tile_rows(place_ref[tile])
        query = qkv_ref[held, at : at + HEAD]
        dout = dout_ref[rows, at : at + HEAD]
        base = (head * tile_count + tile) * slots
        spots = [tile_rows(place_ref[tiles_ref[base + s]]) for s in range(slots)]
        scores = []
        for s in range(slots):
            key = qkv_ref[spots[s], width + at : width + at + HEAD]
            part = dot(key, query, NT) * scale
            scores.append(jnp.where(live_ref[base + s] > 0, part, -1e30))
        peak = jnp.max(functools.reduce(jnp.maximum, scores), axis=0, keepdims=True)
        grown = [jnp.exp(part - peak) for part in scores]
        total = jnp.sum(functools.reduce(jnp.add, grown), axis=0, keepdims=True)
        inverse = 1.0 / total
        probs = [part * inverse for part in grown]
        probs_bf = jnp.concatenate([part.astype(jnp.bfloat16) for part in probs], axis=0)
        grads = []
        for s in range(slots):
            value = qkv_ref[spots[s], 2 * width + at : 2 * width + at + HEAD]
            grads.append(dot(value, dout, NT))
        delta = functools.reduce(jnp.add, [p * g for p, g in zip(probs, grads)])
        delta = jnp.sum(delta, axis=0, keepdims=True)
        dscores = jnp.concatenate(
            [(p * (g - delta) * scale).astype(jnp.bfloat16) for p, g in zip(probs, grads)], axis=0
        )
        value_t = jnp.concatenate([vt_ref[head, :, spot] for spot in spots], axis=1)
        key_t = jnp.concatenate([kt_ref[head, :, spot] for spot in spots], axis=1)
        out_ref[rows, at : at + HEAD] = dot(value_t, probs_bf, NN).T.astype(jnp.bfloat16)
        dqkv_ref[held, at : at + HEAD] = dot(key_t, dscores, NN).T.astype(jnp.bfloat16)
        dk = dot(dscores, query, NN)
        dv = dot(probs_bf, dout, NN)
        for s in range(slots):
            dk_ref[head, spots[s], :] += dk[s * TILE : (s + 1) * TILE]
            dv_ref[head, spots[s], :] += dv[s * TILE : (s + 1) * TILE]

    def step(tile, carry):
        for head in range(heads):
            one(head, tile)
        return carry

    lax.fori_loop(0, tile_count, step, 0)
    for head in range(heads):
        at = head * HEAD
        dqkv_ref[:, width + at : width + at + HEAD] = dk_ref[head].astype(jnp.bfloat16)
        dqkv_ref[:, 2 * width + at : 2 * width + at + HEAD] = dv_ref[head].astype(jnp.bfloat16)


    half = chunk // 2
    first_ref[...] = dot(dqkv_ref[chunk : chunk + half, :], w_ref[...], NT).astype(jnp.bfloat16)
    second_ref[...] = dot(dqkv_ref[chunk + half : 2 * chunk, :], w_ref[...], NT).astype(jnp.bfloat16)


def attention(early, late, last, w, dout, place, kv_tiles, tile_live, chunk):
    length = dout.shape[0]
    heads, tile_count, slots = kv_tiles.shape
    width = heads * HEAD
    depth = w.shape[0]
    smem = pl.BlockSpec(memory_space=pltpu.SMEM)
    vmem = pl.BlockSpec(memory_space=pltpu.VMEM)
    anywhere = pl.BlockSpec(memory_space=pl.ANY)
    return pl.pallas_call(
        functools.partial(attention_kernel, heads=heads, slots=slots, chunk=chunk),
        out_shape=(
            jax.ShapeDtypeStruct((length, width), jnp.bfloat16),
            jax.ShapeDtypeStruct((length, 3 * width), jnp.bfloat16),
            jax.ShapeDtypeStruct((chunk // 2, depth), jnp.bfloat16),
            jax.ShapeDtypeStruct((chunk // 2, depth), jnp.bfloat16),
        ),
        in_specs=[smem, smem, smem, anywhere, vmem, vmem, vmem, vmem],
        out_specs=(vmem, vmem, vmem, vmem),
        scratch_shapes=[
            pltpu.VMEM((length, 3 * width), jnp.bfloat16),
            pltpu.VMEM((heads, HEAD, length), jnp.bfloat16),
            pltpu.VMEM((heads, HEAD, length), jnp.bfloat16),
            pltpu.VMEM((heads, length, HEAD), jnp.float32),
            pltpu.VMEM((heads, length, HEAD), jnp.float32),
            pltpu.SemaphoreType.DMA,
        ],
        name="attention",
        cost_estimate=pl.CostEstimate(
            flops=12 * heads * tile_count * slots * TILE * TILE * HEAD,
            bytes_accessed=16 * length * width,
            transcendentals=heads * tile_count * slots * TILE * TILE,
        ),
        compiler_params=pltpu.CompilerParams(vmem_limit_bytes=26 << 20),
    )(place, kv_tiles.reshape(-1), tile_live.reshape(-1), early, late, last, w, dout)


def folded(count):
    return list(range(0, count, 2)) + list(range(count - 1 - count % 2, 0, -2))


def weight_bits(count):
    return [1 << b for b in range(1, count.bit_length() - 1)]


def gather_weights(w, axis, count):
    half = w.shape[0] // 2

    def swap(value, bit):
        return lax.ppermute(value, axis, [(i, i ^ bit) for i in range(count)])

    held = {0: w}
    bits = weight_bits(count)
    if len(bits) == 2:
        low, high = bits
        held[low] = swap(w, low)
        held[high] = swap(w, high)
        held[low | high] = jnp.concatenate(
            [swap(held[high][:half], low), swap(held[low][half:], high)],
            axis=0,
        )
    else:
        for bit in bits:
            held.update({k | bit: swap(v, bit) for k, v in list(held.items())})
    keys = list(held)
    for k in keys:
        held[k ^ 1] = swap(held[k], 1)
    return held


def make_shards(fsdp_count, sp_count):
    order = folded(sp_count)
    ring = [(order[i], order[(i + 1) % sp_count]) for i in range(sp_count)]
    spot = [order.index(z) for z in range(sp_count)]
    arrived = [[(spot[z] - spot[c]) % sp_count for c in range(sp_count)] for z in range(sp_count)]

    def layer(tokens_in, w_qkv, grad_attn, kv_tiles, tile_live):
        tokens = tokens_in[0]
        chunk, _ = tokens.shape
        half = chunk // 2
        heads, tile_count, _ = kv_tiles.shape
        length = tile_count * TILE
        width = heads * HEAD
        held = gather_weights(w_qkv.reshape(w_qkv.shape[0], -1), "fsdp", fsdp_count)
        halves = [tokens[:half], tokens[half:]]
        parts = [tokens]
        for _ in range(1, sp_count):
            for side in range(2):
                halves[side] = lax.ppermute(halves[side], "sp", ring)
                parts.append(halves[side])
        owners = lax.axis_index("fsdp") ^ jnp.array(list(held), jnp.int32)
        w, early = project(owners, list(held.values()), parts[:-2])
        per_chunk = chunk // TILE
        steps = jnp.array(arrived, jnp.int32)[lax.axis_index("sp")]
        tiles = jnp.arange(tile_count, dtype=jnp.int32)
        place = jnp.repeat(steps, per_chunk) * per_chunk + tiles % per_chunk
        out, dqkv, low, high = attention(
            early, parts[-2], parts[-1], w, grad_attn[0].reshape(length, width), place, kv_tiles, tile_live, chunk
        )
        sums = products(dqkv, w, 2 * chunk, [half] * (2 * (sp_count - 2)) + [chunk])
        for step in range(1, sp_count):
            if step > 1:
                low = (sums[2 * step - 4] + low.astype(jnp.float32)).astype(jnp.bfloat16)
            low = lax.ppermute(low, "sp", ring)
            if step > 1:
                high = (sums[2 * step - 3] + high.astype(jnp.float32)).astype(jnp.bfloat16)
            high = lax.ppermute(high, "sp", ring)
        grad_tokens = finish(sums[-1], low, high)
        return out.reshape(1, length, heads, HEAD), grad_tokens[None]

    return layer


def solution(mesh):
    in_specs = (
        P("fsdp", "sp", None),
        P("fsdp", None, "sp", None),
        P("fsdp", None, "sp", None),
        P("sp", None, None),
        P("sp", None, None),
    )
    out_specs = (P("fsdp", None, "sp", None), P("fsdp", "sp", None))
    shards = make_shards(mesh.shape["fsdp"], mesh.shape["sp"])
    return jax.shard_map(shards, mesh=mesh, in_specs=in_specs, out_specs=out_specs, check_vma=False)
```

```python
import functools

import jax
import jax.numpy as jnp
from jax import lax
from jax.experimental import pallas as pl
from jax.experimental.pallas import tpu as pltpu
from jax.sharding import PartitionSpec as P


HEAD = 128
TILE = 128
NN = (((1,), (0,)), ((), ()))
NT = (((1,), (1,)), ((), ()))


PAUSE = 4400
LOG2E = 1.4426950408889634


def dot(a, b, dims):
    return lax.dot_general(a, b, dims, preferred_element_type=jnp.float32)


def weave(*streams):
    streams = [stream for stream in streams if stream is not None]
    while streams:
        streams = [stream for stream in streams if next(stream, None) is not None]


def project_kernel(*refs, keys, parts):
    shards = len(keys)
    mine = lax.axis_index("fsdp")
    shard_refs, part_refs = refs[:shards], refs[shards : shards + parts]
    w_ref, qkv_ref, sems = refs[shards + parts :]
    rows = shard_refs[0].shape[0]
    copies = []
    for number, shard in enumerate(shard_refs):
        at = pl.ds(pl.multiple_of((mine ^ keys[number]) * rows, rows), rows)
        copies.append(pltpu.make_async_copy(shard, w_ref.at[at], sems.at[number]))
    for copy in copies:
        copy.start()
    for copy in copies:
        copy.wait()
    start = 0
    for part in part_refs:
        size = part.shape[0]
        qkv_ref[start : start + size, :] = dot(part[...], w_ref[...], NN).astype(jnp.bfloat16)
        start += size


def project(keys, shards, parts):
    _, width = shards[0].shape
    depth = parts[0].shape[1]
    length = sum(part.shape[0] for part in parts)
    anywhere = pl.BlockSpec(memory_space=pl.ANY)
    return pl.pallas_call(
        functools.partial(project_kernel, keys=tuple(keys), parts=len(parts)),
        out_shape=(
            jax.ShapeDtypeStruct((depth, width), jnp.bfloat16),
            jax.ShapeDtypeStruct((length, width), jnp.bfloat16),
        ),
        in_specs=[anywhere] * len(shards) + [pl.BlockSpec(memory_space=pltpu.VMEM)] * len(parts),
        out_specs=(pl.BlockSpec(memory_space=pltpu.VMEM),) * 2,
        scratch_shapes=[pltpu.SemaphoreType.DMA((len(shards),))],
        name="project",
        cost_estimate=pl.CostEstimate(
            flops=2 * length * depth * width,
            bytes_accessed=4 * depth * width + 4 * length * width,
            transcendentals=0,
        ),
        compiler_params=pltpu.CompilerParams(vmem_limit_bytes=16 << 20),
    )(*shards, *parts)


def product_kernel(dqkv_ref, w_ref, *out_refs, start):
    for out_ref in out_refs:
        rows = out_ref.shape[0]
        start = start % dqkv_ref.shape[0]
        out_ref[...] = dot(dqkv_ref[start : start + rows, :], w_ref[...], NT).astype(out_ref.dtype)
        start += rows


def products(dqkv, w, start, sizes, dtype=jnp.float32):
    depth, width = w.shape
    return pl.pallas_call(
        functools.partial(product_kernel, start=start),
        out_shape=tuple(jax.ShapeDtypeStruct((size, depth), dtype) for size in sizes),
        name="products",
        cost_estimate=pl.CostEstimate(
            flops=2 * sum(sizes) * depth * width,
            bytes_accessed=2 * depth * width + 6 * sum(sizes) * depth,
            transcendentals=0,
        ),
        compiler_params=pltpu.CompilerParams(vmem_limit_bytes=12 << 20),
    )(dqkv, w)


def finish_kernel(own_ref, low_ref, high_ref, out_ref):
    half = low_ref.shape[0]
    out_ref[:half, :] = (own_ref[:half, :] + low_ref[...].astype(jnp.float32)).astype(jnp.bfloat16)
    out_ref[half:, :] = (own_ref[half:, :] + high_ref[...].astype(jnp.float32)).astype(jnp.bfloat16)


def finish(own, low, high):
    return pl.pallas_call(
        finish_kernel,
        out_shape=jax.ShapeDtypeStruct(own.shape, jnp.bfloat16),
        name="finish",
        compiler_params=pltpu.CompilerParams(vmem_limit_bytes=8 << 20),
    )(own, low, high)


def attention_kernel(
    code_ref, early_ref, late_ref, last_ref, w_ref, dout_ref,
    out_ref, dqkv_ref, first_ref, place_ref, qkv_ref, kt_ref, vt_ref, *refs,
    heads, slots, chunk,
):
    dkv_refs, score_refs, grad_refs, prob_refs, peak_refs = (
        refs[group * heads : (group + 1) * heads] for group in range(5)
    )
    sem = refs[5 * heads]
    length = qkv_ref.shape[0]
    width = heads * HEAD
    tile_count = length // TILE
    scale = HEAD ** (-0.5)
    per_chunk = chunk // TILE
    sp_count = length // chunk
    device = lax.axis_index("sp")
    spot = jnp.where(device % 2 == 0, device // 2, sp_count - 1 - device // 2)
    for number in range(sp_count):
        step = lax.rem(spot - ring_spot(number, sp_count) + sp_count, sp_count)
        for tile in range(per_chunk):
            place_ref[number * per_chunk + tile] = step * per_chunk + tile
    early = early_ref.shape[0]
    middle_row = early + late_ref.shape[0]
    copy = pltpu.make_async_copy(early_ref, qkv_ref.at[pl.ds(0, early)], sem)
    copy.start()
    qkv_ref[early:middle_row, :] = dot(late_ref[...], w_ref[...], NN).astype(jnp.bfloat16)
    qkv_ref[middle_row:, :] = dot(last_ref[...], w_ref[...], NN).astype(jnp.bfloat16)
    for head in range(heads):
        dkv_refs[head][...] = jnp.zeros_like(dkv_refs[head])
    copy.wait()
    for head in range(heads):
        at = head * HEAD
        kt_ref[head] = qkv_ref[:, width + at : width + at + HEAD].T
        vt_ref[head] = qkv_ref[:, 2 * width + at : 2 * width + at + HEAD].T

    def tile_rows(tile):
        return pl.ds(pl.multiple_of(tile * TILE, TILE), TILE)

    def spots_of(head, tile):
        base = (head * tile_count + tile) * slots
        return base, [tile_rows(place_ref[jnp.maximum(code_ref[base + s], 0)]) for s in range(slots)]

    def operands(head, tile):
        at = head * HEAD
        query = qkv_ref[tile_rows(place_ref[tile]), at : at + HEAD]
        return query, dout_ref[tile_rows(tile), at : at + HEAD]

    def enter(head, tile):
        at = head * HEAD
        base, spots = spots_of(head, tile)
        query, dout = operands(head, tile)
        peak = None
        empty = jnp.zeros((TILE, HEAD), jnp.bfloat16)
        both = jnp.concatenate([jnp.concatenate([query, empty], axis=1), jnp.concatenate([empty, dout], axis=1)], axis=0)
        for s in range(slots):
            key = qkv_ref[spots[s], width + at : width + at + HEAD]
            value = qkv_ref[spots[s], 2 * width + at : 2 * width + at + HEAD]
            part = dot(jnp.concatenate([key, value], axis=1), both, NT)
            score = part[:, :TILE]
            if s > 0:
                score = jnp.where(code_ref[base + s] >= 0, score, -1e30)
            score_refs[head][s * TILE : (s + 1) * TILE, :] = score
            grad_refs[head][s * TILE : (s + 1) * TILE, :] = part[:, TILE:]
            peak = score if peak is None else jnp.maximum(peak, score)
            yield True
            yield True
        peak_refs[head][...] = jnp.broadcast_to(jnp.max(peak, axis=0, keepdims=True), (8, TILE))

    def middle(head, tile):
        peak = peak_refs[head][:1, :]
        total = jnp.zeros((1, TILE), jnp.float32)
        delta = jnp.zeros((1, TILE), jnp.float32)
        for s in range(slots):
            part = slice(s * TILE, (s + 1) * TILE)
            grown = jnp.exp2((score_refs[head][part, :] - peak) * (scale * LOG2E))
            score_refs[head][part, :] = grown
            total += jnp.sum(grown, axis=0, keepdims=True)
            delta += jnp.sum(grown * grad_refs[head][part, :], axis=0, keepdims=True)
            yield True
        inverse = 1.0 / total
        delta = delta * inverse
        for s in range(slots):
            part = slice(s * TILE, (s + 1) * TILE)
            prob = score_refs[head][part, :] * inverse
            prob_refs[head][part, TILE:] = prob.astype(jnp.bfloat16)
            prob_refs[head][part, :TILE] = (prob * (grad_refs[head][part, :] - delta) * scale).astype(jnp.bfloat16)
            yield True

    def leave(head, tile):
        at = head * HEAD
        rows = tile_rows(tile)
        held = tile_rows(place_ref[tile])
        _, spots = spots_of(head, tile)
        query, dout = operands(head, tile)
        empty = jnp.zeros((TILE, HEAD), jnp.bfloat16)
        both = jnp.concatenate([jnp.concatenate([query, empty], axis=1), jnp.concatenate([empty, dout], axis=1)], axis=0)
        value_t = jnp.concatenate([vt_ref[head, :, spot] for spot in spots], axis=1)
        out_ref[rows, at : at + HEAD] = dot(value_t, prob_refs[head][:, TILE:], NN).T.astype(jnp.bfloat16)
        yield True
        key_t = jnp.concatenate([kt_ref[head, :, spot] for spot in spots], axis=1)
        dqkv_ref[held, at : at + HEAD] = dot(key_t, prob_refs[head][:, :TILE], NN).T.astype(jnp.bfloat16)
        yield True
        for s in range(slots):
            part = slice(s * TILE, (s + 1) * TILE)
            dkv_refs[head][spots[s], :] += dot(prob_refs[head][part, :], both, NN)
            yield True

    def before(head, tile, back):
        order = head - back
        return (order % heads, tile + order // heads)

    def turn(tile, first):
        for head in range(heads):
            weave(
                enter(head, tile),
                middle(*before(head, tile, 1)) if not first or head >= 1 else None,
                leave(*before(head, tile, 2)) if not first or head >= 2 else None,
            )

    turn(0, True)

    def step(tile, carry):
        turn(tile, False)
        return carry

    lax.fori_loop(1, tile_count, step, 0)
    weave(middle(heads - 1, tile_count - 1), leave(*before(heads, tile_count - 1, 2)))
    weave(leave(heads - 1, tile_count - 1))
    for head in range(heads):
        at = head * HEAD
        dqkv_ref[:, width + at : width + at + HEAD] = dkv_refs[head][:, :HEAD].astype(jnp.bfloat16)
        dqkv_ref[:, 2 * width + at : 2 * width + at + HEAD] = dkv_refs[head][:, HEAD:].astype(jnp.bfloat16)
    half = chunk // 2
    first_ref[...] = dot(dqkv_ref[chunk : chunk + half, :], w_ref[...], NT).astype(jnp.bfloat16)


def attention(early, late, last, w, dout, codes, chunk):
    length = dout.shape[0]
    heads, tile_count, slots = codes.shape
    width = heads * HEAD
    depth = w.shape[0]
    smem = pl.BlockSpec(memory_space=pltpu.SMEM)
    vmem = pl.BlockSpec(memory_space=pltpu.VMEM)
    anywhere = pl.BlockSpec(memory_space=pl.ANY)
    return pl.pallas_call(
        functools.partial(attention_kernel, heads=heads, slots=slots, chunk=chunk),
        out_shape=(
            jax.ShapeDtypeStruct((length, width), jnp.bfloat16),
            jax.ShapeDtypeStruct((length, 3 * width), jnp.bfloat16),
            jax.ShapeDtypeStruct((chunk // 2, depth), jnp.bfloat16),
        ),
        in_specs=[smem, anywhere, vmem, vmem, vmem, vmem],
        out_specs=(vmem, vmem, vmem),
        scratch_shapes=[
            pltpu.SMEM((tile_count,), jnp.int32),
            pltpu.VMEM((length, 3 * width), jnp.bfloat16),
            pltpu.VMEM((heads, HEAD, length), jnp.bfloat16),
            pltpu.VMEM((heads, HEAD, length), jnp.bfloat16),
        ]
        + [pltpu.VMEM((length, 2 * HEAD), jnp.float32)] * heads
        + [pltpu.VMEM((slots * TILE, TILE), jnp.float32)] * (2 * heads)
        + [pltpu.VMEM((slots * TILE, 2 * TILE), jnp.bfloat16)] * heads
        + [pltpu.VMEM((8, TILE), jnp.float32)] * heads
        + [pltpu.SemaphoreType.DMA],
        name="attention",
        cost_estimate=pl.CostEstimate(
            flops=12 * heads * tile_count * slots * TILE * TILE * HEAD,
            bytes_accessed=16 * length * width,
            transcendentals=heads * tile_count * slots * TILE * TILE,
        ),
        compiler_params=pltpu.CompilerParams(vmem_limit_bytes=26 << 20),
    )(codes.reshape(-1), early, late, last, w, dout)


def stagger_kernel(out_ref):
    turns = (lax.axis_index("fsdp") % 2) * PAUSE
    out_ref[0] = lax.fori_loop(0, turns, lambda _, x: (x * 5 + 3) & 1023, turns)


def stagger():
    return pl.pallas_call(
        stagger_kernel,
        out_shape=jax.ShapeDtypeStruct((1,), jnp.int32),
        out_specs=pl.BlockSpec(memory_space=pltpu.SMEM),
        name="stagger",
        compiler_params=pltpu.CompilerParams(has_side_effects=True),
    )()


def ring_spot(device, count):
    return device // 2 if device % 2 == 0 else count - 1 - device // 2


def weight_bits(count):
    return [1 << b for b in range(1, count.bit_length() - 1)]


def gather_weights(w, axis, count):
    def swap(value, bit):
        return lax.ppermute(value, axis, [(i, i ^ bit) for i in range(count)])

    held = {0: w, 1: swap(w, 1)}
    bits = weight_bits(count)
    if len(bits) == 2:
        low, high = bits
        for k in range(2):
            held[low | k] = swap(held[k], low)
            held[high | k] = swap(held[k], high)
        held[low | high] = swap(held[high], low)
        held[low | high | 1] = swap(held[low | 1], high)
    else:
        for bit in bits:
            held.update({k | bit: swap(v, bit) for k, v in list(held.items())})
    return held


def make_shards(fsdp_count, sp_count):
    order = sorted(range(sp_count), key=lambda device: ring_spot(device, sp_count))
    ring = [(order[i], order[(i + 1) % sp_count]) for i in range(sp_count)]

    def layer(tokens_in, w_qkv, grad_attn, kv_tiles, tile_live):
        tokens = tokens_in[0]
        chunk, _ = tokens.shape
        half = chunk // 2
        heads, tile_count, _ = kv_tiles.shape
        length = tile_count * TILE
        width = heads * HEAD
        codes = jnp.where(tile_live > 0, kv_tiles, -1)
        dout = grad_attn[0].reshape(length, width)
        held = gather_weights(w_qkv.reshape(w_qkv.shape[0], -1), "fsdp", fsdp_count)
        halves = [tokens[:half], tokens[half:]]
        parts = [tokens]
        for _ in range(1, sp_count):
            for side in range(2):
                halves[side] = lax.ppermute(halves[side], "sp", ring)
                parts.append(halves[side])
        stagger()
        w, early = project(list(held), list(held.values()), parts[:-2])
        out, dqkv, low = attention(
            early, parts[-2], parts[-1], w, dout, codes, chunk
        )
        (high,) = products(dqkv, w, chunk + half, [half], jnp.bfloat16)
        sums = []
        for step in range(2, sp_count):
            sums += products(dqkv, w, step * chunk, [half, half])
        sums += products(dqkv, w, 0, [chunk])
        for step in range(1, sp_count):
            if step > 1:
                low = (sums[2 * step - 4] + low.astype(jnp.float32)).astype(jnp.bfloat16)
            low = lax.ppermute(low, "sp", ring)
            if step > 1:
                high = (sums[2 * step - 3] + high.astype(jnp.float32)).astype(jnp.bfloat16)
            high = lax.ppermute(high, "sp", ring)
        grad_tokens = finish(sums[-1], low, high)
        out = out.reshape(1, length, heads, HEAD)
        return out, grad_tokens[None]

    return layer


def solution(mesh):
    in_specs = (
        P("fsdp", "sp", None),
        P("fsdp", None, "sp", None),
        P("fsdp", None, "sp", None),
        P("sp", None, None),
        P("sp", None, None),
    )
    out_specs = (P("fsdp", None, "sp", None), P("fsdp", "sp", None))
    shards = make_shards(mesh.shape["fsdp"], mesh.shape["sp"])
    return jax.shard_map(shards, mesh=mesh, in_specs=in_specs, out_specs=out_specs, check_vma=False)
```

```python
import functools

import jax
import jax.numpy as jnp
from jax import lax
from jax.experimental import pallas as pl
from jax.experimental.pallas import tpu as pltpu
from jax.sharding import PartitionSpec as P


HEAD = 128
TILE = 128
NN = (((1,), (0,)), ((), ()))
NT = (((1,), (1,)), ((), ()))


PAUSE = 4400
LOG2E = 1.4426950408889634


def dot(a, b, dims):
    return lax.dot_general(a, b, dims, preferred_element_type=jnp.float32)


def groups(slots):
    return [range(s, min(s + 2, slots)) for s in range(0, slots, 2)]


def weave(*streams):
    streams = [stream for stream in streams if stream is not None]
    while streams:
        streams = [stream for stream in streams if next(stream, None) is not None]


def project_kernel(*refs, keys, parts):
    shards = len(keys)
    mine = lax.axis_index("fsdp")
    shard_refs, part_refs = refs[:shards], refs[shards : shards + parts]
    w_ref, qkv_ref = refs[shards + parts :]
    rows, width = shard_refs[0].shape
    block = 4 * HEAD

    def fill(column):
        for place, shard in enumerate(shard_refs):
            at = pl.ds(pl.multiple_of((mine ^ keys[place]) * rows, rows), rows)
            w_ref[at, column : column + block] = shard[:, column : column + block]
            yield True

    def multiply(column):
        tokens = jnp.concatenate([part[...] for part in part_refs], axis=0)
        columns = slice(column, column + block)
        qkv_ref[:, columns] = dot(tokens, w_ref[:, columns], NN).astype(jnp.bfloat16)
        yield True

    weave(fill(0))
    for column in range(0, width, block):
        weave(fill(column + block) if column + block < width else None, multiply(column))


def project(keys, shards, parts):
    _, width = shards[0].shape
    depth = parts[0].shape[1]
    length = sum(part.shape[0] for part in parts)
    anywhere = pl.BlockSpec(memory_space=pl.ANY)
    return pl.pallas_call(
        functools.partial(project_kernel, keys=tuple(keys), parts=len(parts)),
        out_shape=(
            jax.ShapeDtypeStruct((depth, width), jnp.bfloat16),
            jax.ShapeDtypeStruct((length, width), jnp.bfloat16),
        ),
        in_specs=[pl.BlockSpec(memory_space=pltpu.VMEM)] * (len(shards) + len(parts)),
        out_specs=(pl.BlockSpec(memory_space=pltpu.VMEM),) * 2,
        name="project",
        cost_estimate=pl.CostEstimate(
            flops=2 * length * depth * width,
            bytes_accessed=4 * depth * width + 4 * length * width,
            transcendentals=0,
        ),
        compiler_params=pltpu.CompilerParams(vmem_limit_bytes=max(4 << 20, (2 << 20) + 2 * length * depth)),
    )(*shards, *parts)


def product_kernel(dqkv_ref, w_ref, *out_refs, start):
    def multiply(start, out_refs):
        rows = sum(out_ref.shape[0] for out_ref in out_refs)
        whole = dot(dqkv_ref[start : start + rows, :], w_ref[...], NT)
        at = 0
        for out_ref in out_refs:
            out_ref[...] = whole[at : at + out_ref.shape[0]]
            at += out_ref.shape[0]

    for number in range(0, len(out_refs) - 1, 2):
        multiply(start, out_refs[number : number + 2])
        start += 2 * out_refs[number].shape[0]
    multiply(0, out_refs[-1:])


def products(dqkv, w, start, sizes):
    depth, width = w.shape
    return pl.pallas_call(
        functools.partial(product_kernel, start=start),
        out_shape=tuple(jax.ShapeDtypeStruct((size, depth), jnp.float32) for size in sizes),
        name="products",
        cost_estimate=pl.CostEstimate(
            flops=2 * sum(sizes) * depth * width,
            bytes_accessed=2 * depth * width + 6 * sum(sizes) * depth,
            transcendentals=0,
        ),
        compiler_params=pltpu.CompilerParams(vmem_limit_bytes=4 << 20),
    )(dqkv, w)


def finish_kernel(own_ref, low_ref, high_ref, out_ref):
    half = low_ref.shape[0]
    out_ref[:half, :] = (own_ref[:half, :] + low_ref[...].astype(jnp.float32)).astype(jnp.bfloat16)
    out_ref[half:, :] = (own_ref[half:, :] + high_ref[...].astype(jnp.float32)).astype(jnp.bfloat16)


def finish(own, low, high):
    return pl.pallas_call(
        finish_kernel,
        out_shape=jax.ShapeDtypeStruct(own.shape, jnp.bfloat16),
        name="finish",
        compiler_params=pltpu.CompilerParams(vmem_limit_bytes=2 << 20),
    )(own, low, high)


def attention_kernel(
    packed_ref, early_ref, late_ref, last_ref, w_ref, dout_ref,
    out_ref, dqkv_ref, first_ref, second_ref, place_ref, qkv_ref, kt_ref, vt_ref, *refs,
    heads, all_slots, chunk,
):
    dkv_refs, score_refs, grad_refs, prob_refs, peak_refs = (
        refs[group * heads : (group + 1) * heads] for group in range(5)
    )
    sem = refs[5 * heads]
    length = qkv_ref.shape[0]
    width = heads * HEAD
    tile_count = length // TILE
    scale = HEAD ** (-0.5)
    early = early_ref.shape[0]
    copy = pltpu.make_async_copy(early_ref, qkv_ref.at[pl.ds(0, early)], sem)
    copy.start()
    per_chunk = chunk // TILE
    sp_count = length // chunk
    device = lax.axis_index("sp")
    spot = jnp.where(device % 2 == 0, device // 2, sp_count - 1 - device // 2)
    for number in range(sp_count):
        step = lax.rem(spot - ring_spot(number, sp_count) + sp_count, sp_count)
        for tile in range(per_chunk):
            place_ref[number * per_chunk + tile] = step * per_chunk + tile
    most = packed_ref[heads * tile_count * all_slots]

    def project_late():
        for column in range(0, 3 * width, 2 * HEAD):
            columns = slice(column, column + 2 * HEAD)
            tokens = jnp.concatenate([late_ref[...], last_ref[...]], axis=0)
            qkv_ref[early:, columns] = dot(tokens, w_ref[:, columns], NN).astype(jnp.bfloat16)
            yield True

    def turn_rows(start, stop):
        for head in range(heads):
            at = head * HEAD
            for row in range(start, stop, TILE):
                rows = slice(row, row + TILE)
                kt_ref[head, :, rows] = qkv_ref[rows, width + at : width + at + HEAD].T
                vt_ref[head, :, rows] = qkv_ref[rows, 2 * width + at : 2 * width + at + HEAD].T
                yield True

    def clear():
        for head in range(heads):
            for row in range(0, length, TILE):
                dkv_refs[head][row : row + TILE, :] = jnp.zeros((TILE, 2 * HEAD), jnp.float32)
                yield True

    weave(clear())
    copy.wait()
    weave(project_late(), turn_rows(0, early))
    weave(turn_rows(early, length))

    def tile_rows(tile):
        return pl.ds(pl.multiple_of(tile * TILE, TILE), TILE)

    def spots_of(head, tile, slots):
        base = (head * tile_count + tile) * all_slots
        return base, [tile_rows(place_ref[jnp.maximum(packed_ref[base + s], 0)]) for s in range(slots)]

    def operands(head, tile):
        at = head * HEAD
        query = qkv_ref[tile_rows(place_ref[tile]), at : at + HEAD]
        return query, dout_ref[tile_rows(tile), at : at + HEAD]

    def enter(slots, head, tile):
        at = head * HEAD
        base, spots = spots_of(head, tile, slots)
        query, dout = operands(head, tile)
        peak = None
        empty = jnp.zeros((TILE, HEAD), jnp.bfloat16)
        both = jnp.concatenate([jnp.concatenate([query, empty], axis=1), jnp.concatenate([empty, dout], axis=1)], axis=0)
        for group in groups(slots):
            lhs = [
                jnp.concatenate(
                    [
                        qkv_ref[spots[s], width + at : width + at + HEAD],
                        qkv_ref[spots[s], 2 * width + at : 2 * width + at + HEAD],
                    ],
                    axis=1,
                )
                for s in group
            ]
            parts = dot(jnp.concatenate(lhs, axis=0), both, NT)
            yield True
            for number, s in enumerate(group):
                part = parts[number * TILE : (number + 1) * TILE]
                score = part[:, :TILE]
                if s > 0:
                    score = jnp.where(packed_ref[base + s] >= 0, score, -1e30)
                score_refs[head][s * TILE : (s + 1) * TILE, :] = score
                grad_refs[head][s * TILE : (s + 1) * TILE, :] = part[:, TILE:]
                peak = score if peak is None else jnp.maximum(peak, score)
                yield True
        peak_refs[head][...] = jnp.broadcast_to(jnp.max(peak, axis=0, keepdims=True), (8, TILE))

    def middle(slots, head, tile):
        peak = peak_refs[head][:1, :]
        total = jnp.zeros((1, TILE), jnp.float32)
        delta = jnp.zeros((1, TILE), jnp.float32)
        for s in range(slots):
            part = slice(s * TILE, (s + 1) * TILE)
            grown = jnp.exp2((score_refs[head][part, :] - peak) * (scale * LOG2E))
            score_refs[head][part, :] = grown
            total += jnp.sum(grown, axis=0, keepdims=True)
            delta += jnp.sum(grown * grad_refs[head][part, :], axis=0, keepdims=True)
            yield True
        inverse = 1.0 / total
        delta = delta * inverse
        for s in range(slots):
            part = slice(s * TILE, (s + 1) * TILE)
            prob = score_refs[head][part, :] * inverse
            prob_refs[head][part, TILE:] = prob.astype(jnp.bfloat16)
            prob_refs[head][part, :TILE] = (prob * (grad_refs[head][part, :] - delta) * scale).astype(jnp.bfloat16)
            yield True

    def leave(slots, head, tile):
        at = head * HEAD
        rows = tile_rows(tile)
        held = tile_rows(place_ref[tile])
        _, spots = spots_of(head, tile, slots)
        query, dout = operands(head, tile)
        empty = jnp.zeros((TILE, HEAD), jnp.bfloat16)
        both = jnp.concatenate([jnp.concatenate([query, empty], axis=1), jnp.concatenate([empty, dout], axis=1)], axis=0)
        value_t = jnp.concatenate([vt_ref[head, :, spot] for spot in spots], axis=1)
        out_ref[rows, at : at + HEAD] = dot(value_t, prob_refs[head][: slots * TILE, TILE:], NN).T.astype(jnp.bfloat16)
        yield True
        key_t = jnp.concatenate([kt_ref[head, :, spot] for spot in spots], axis=1)
        dqkv_ref[held, at : at + HEAD] = dot(key_t, prob_refs[head][: slots * TILE, :TILE], NN).T.astype(jnp.bfloat16)
        yield True
        for group in groups(slots):
            parts = dot(prob_refs[head][group[0] * TILE : (group[-1] + 1) * TILE, :], both, NN)
            yield True
            for number, s in enumerate(group):
                dkv_refs[head][spots[s], :] += parts[number * TILE : (number + 1) * TILE]
                yield True

    def before(head, tile, back):
        order = head - back
        return (order % heads, tile + order // heads)

    def turn(slots, tile, first):
        for head in range(heads):
            weave(
                enter(slots, head, tile),
                middle(slots, *before(head, tile, 1)) if not first or head >= 1 else None,
                leave(slots, *before(head, tile, 2)) if not first or head >= 2 else None,
            )

    def run(slots):
        turn(slots, 0, True)

        def step(tile, carry):
            turn(slots, tile, False)
            return carry

        lax.fori_loop(1, tile_count, step, 0)
        last = tile_count - 1
        weave(middle(slots, heads - 1, last), leave(slots, *before(heads, last, 2)))
        weave(leave(slots, heads - 1, last))

    few = all_slots - 1
    if few > 0:
        pl.when(most <= few)(lambda: run(few))
        pl.when(most > few)(lambda: run(all_slots))
    else:
        run(all_slots)
    for head in range(heads):
        at = head * HEAD
        dqkv_ref[:, width + at : width + at + HEAD] = dkv_refs[head][:, :HEAD].astype(jnp.bfloat16)
        dqkv_ref[:, 2 * width + at : 2 * width + at + HEAD] = dkv_refs[head][:, HEAD:].astype(jnp.bfloat16)
    half = chunk // 2
    whole = dot(dqkv_ref[chunk : 2 * chunk, :], w_ref[...], NT).astype(jnp.bfloat16)
    first_ref[...] = whole[:half]
    second_ref[...] = whole[half:]


def attention(early, late, last, w, dout, codes, shape, chunk):
    length = dout.shape[0]
    heads, tile_count, slots = shape
    width = heads * HEAD
    depth = w.shape[0]
    smem = pl.BlockSpec(memory_space=pltpu.SMEM)
    vmem = pl.BlockSpec(memory_space=pltpu.VMEM)
    anywhere = pl.BlockSpec(memory_space=pl.ANY)
    return pl.pallas_call(
        functools.partial(attention_kernel, heads=heads, all_slots=slots, chunk=chunk),
        out_shape=(
            jax.ShapeDtypeStruct((length, width), jnp.bfloat16),
            jax.ShapeDtypeStruct((length, 3 * width), jnp.bfloat16),
            jax.ShapeDtypeStruct((chunk // 2, depth), jnp.bfloat16),
            jax.ShapeDtypeStruct((chunk // 2, depth), jnp.bfloat16),
        ),
        in_specs=[smem, anywhere, vmem, vmem, vmem, vmem],
        out_specs=(vmem, vmem, vmem, vmem),
        scratch_shapes=[
            pltpu.SMEM((tile_count,), jnp.int32),
            pltpu.VMEM((length, 3 * width), jnp.bfloat16),
            pltpu.VMEM((heads, HEAD, length), jnp.bfloat16),
            pltpu.VMEM((heads, HEAD, length), jnp.bfloat16),
        ]
        + [pltpu.VMEM((length, 2 * HEAD), jnp.float32)] * heads
        + [pltpu.VMEM((slots * TILE, TILE), jnp.float32)] * (2 * heads)
        + [pltpu.VMEM((slots * TILE, 2 * TILE), jnp.bfloat16)] * heads
        + [pltpu.VMEM((8, TILE), jnp.float32)] * heads
        + [pltpu.SemaphoreType.DMA],
        name="attention",
        cost_estimate=pl.CostEstimate(
            flops=12 * heads * tile_count * slots * TILE * TILE * HEAD,
            bytes_accessed=16 * length * width,
            transcendentals=heads * tile_count * slots * TILE * TILE,
        ),
        compiler_params=pltpu.CompilerParams(vmem_limit_bytes=18 << 20),
    )(codes, early, late, last, w, dout)


def pack_kernel(code_ref, dout_ref, packed_ref, *, slots):
    rows = code_ref.shape[0] // slots
    most = 1
    for base in range(0, rows * slots, slots):
        packed = [code_ref[base]] + [-1] * (slots - 1)
        count = 1
        for s in range(1, slots):
            code = code_ref[base + s]
            target = jnp.where(code >= 0, count, 0)
            for j in range(1, s + 1):
                packed[j] = jnp.where(target == j, code, packed[j])
            count = count + jnp.where(code >= 0, 1, 0)
        for s in range(slots):
            packed_ref[base + s] = packed[s]
        most = jnp.maximum(most, count)
    packed_ref[rows * slots] = most


def pack(codes, slots, dout):
    smem = pl.BlockSpec(memory_space=pltpu.SMEM)
    return pl.pallas_call(
        functools.partial(pack_kernel, slots=slots),
        out_shape=jax.ShapeDtypeStruct((codes.shape[0] + 1,), jnp.int32),
        in_specs=[smem, pl.BlockSpec(memory_space=pl.ANY)],
        out_specs=smem,
        name="pack",
        compiler_params=pltpu.CompilerParams(vmem_limit_bytes=1 << 20),
    )(codes, dout)


def stagger_kernel(out_ref):
    turns = (lax.axis_index("fsdp") % 2) * PAUSE
    out_ref[0] = lax.fori_loop(0, turns, lambda _, x: (x * 5 + 3) & 1023, turns)


def stagger():
    return pl.pallas_call(
        stagger_kernel,
        out_shape=jax.ShapeDtypeStruct((1,), jnp.int32),
        out_specs=pl.BlockSpec(memory_space=pltpu.SMEM),
        name="stagger",
        compiler_params=pltpu.CompilerParams(has_side_effects=True),
    )()


def ring_spot(device, count):
    return device // 2 if device % 2 == 0 else count - 1 - device // 2


def weight_bits(count):
    return [1 << b for b in range(1, count.bit_length() - 1)]


def gather_weights(w, axis, count):
    def swap(value, bit):
        return lax.ppermute(value, axis, [(i, i ^ bit) for i in range(count)])

    held = {0: w, 1: swap(w, 1)}
    bits = weight_bits(count)
    if len(bits) == 2:
        low, high = bits
        for k in range(2):
            held[low | k] = swap(held[k], low)
            held[high | k] = swap(held[k], high)
        held[low | high] = swap(held[high], low)
        held[low | high | 1] = swap(held[low | 1], high)
    else:
        for bit in bits:
            held.update({k | bit: swap(v, bit) for k, v in list(held.items())})
    return held


def make_shards(fsdp_count, sp_count):
    order = sorted(range(sp_count), key=lambda device: ring_spot(device, sp_count))
    ring = [(order[i], order[(i + 1) % sp_count]) for i in range(sp_count)]

    def layer(tokens_in, w_qkv, grad_attn, kv_tiles, tile_live):
        tokens = tokens_in[0]
        chunk, _ = tokens.shape
        half = chunk // 2
        heads, tile_count, _ = kv_tiles.shape
        length = tile_count * TILE
        width = heads * HEAD
        codes = jnp.where(tile_live > 0, kv_tiles, -1).reshape(-1)
        dout = grad_attn[0].reshape(length, width)
        codes = pack(codes, kv_tiles.shape[2], dout)
        held = gather_weights(w_qkv.reshape(w_qkv.shape[0], -1), "fsdp", fsdp_count)
        halves = [tokens[:half], tokens[half:]]
        parts = [tokens]
        for _ in range(1, sp_count):
            for side in range(2):
                halves[side] = lax.ppermute(halves[side], "sp", ring)
                parts.append(halves[side])
        stagger()
        w, early = project(list(held), list(held.values()), parts[:-2])
        out, dqkv, low, high = attention(
            early, parts[-2], parts[-1], w, dout, codes, kv_tiles.shape, chunk
        )
        sums = products(dqkv, w, 2 * chunk, [half] * (2 * sp_count - 4) + [chunk])
        for step in range(1, sp_count):
            if step > 1:
                low = (sums[2 * step - 4] + low.astype(jnp.float32)).astype(jnp.bfloat16)
            low = lax.ppermute(low, "sp", ring)
            if step > 1:
                high = (sums[2 * step - 3] + high.astype(jnp.float32)).astype(jnp.bfloat16)
            high = lax.ppermute(high, "sp", ring)
        grad_tokens = finish(sums[-1], low, high)
        out = out.reshape(1, length, heads, HEAD)
        return out, grad_tokens[None]

    return layer


def solution(mesh):
    in_specs = (
        P("fsdp", "sp", None),
        P("fsdp", None, "sp", None),
        P("fsdp", None, "sp", None),
        P("sp", None, None),
        P("sp", None, None),
    )
    out_specs = (P("fsdp", None, "sp", None), P("fsdp", "sp", None))
    shards = make_shards(mesh.shape["fsdp"], mesh.shape["sp"])
    return jax.shard_map(shards, mesh=mesh, in_specs=in_specs, out_specs=out_specs, check_vma=False)
```

```python
import functools

import jax
import jax.numpy as jnp
from jax import lax
from jax.experimental import pallas as pl
from jax.experimental.pallas import tpu as pltpu
from jax.sharding import PartitionSpec as P


HEAD = 128
TILE = 128
NN = (((1,), (0,)), ((), ()))
NT = (((1,), (1,)), ((), ()))


PAUSE = 4400
LOG2E = 1.4426950408889634


def dot(a, b, dims):
    return lax.dot_general(a, b, dims, preferred_element_type=jnp.float32)


def groups(slots):
    return [range(s, min(s + 2, slots)) for s in range(0, slots, 2)]


def weave(*streams):
    streams = [stream for stream in streams if stream is not None]
    while streams:
        streams = [stream for stream in streams if next(stream, None) is not None]


def project_kernel(*refs, keys, parts):
    shards = len(keys)
    mine = lax.axis_index("fsdp")
    shard_refs, part_refs = refs[:shards], refs[shards : shards + parts]
    w_ref, qkv_ref = refs[shards + parts :]
    rows, width = shard_refs[0].shape
    block = 4 * HEAD

    def fill(column):
        for place, shard in enumerate(shard_refs):
            at = pl.ds(pl.multiple_of((mine ^ keys[place]) * rows, rows), rows)
            w_ref[at, column : column + block] = shard[:, column : column + block]
            yield True

    def multiply(column):
        tokens = jnp.concatenate([part[...] for part in part_refs], axis=0)
        columns = slice(column, column + block)
        qkv_ref[:, columns] = dot(tokens, w_ref[:, columns], NN).astype(jnp.bfloat16)
        yield True

    weave(fill(0))
    for column in range(0, width, block):
        weave(fill(column + block) if column + block < width else None, multiply(column))


def project(keys, shards, parts):
    _, width = shards[0].shape
    depth = parts[0].shape[1]
    length = sum(part.shape[0] for part in parts)
    anywhere = pl.BlockSpec(memory_space=pl.ANY)
    return pl.pallas_call(
        functools.partial(project_kernel, keys=tuple(keys), parts=len(parts)),
        out_shape=(
            jax.ShapeDtypeStruct((depth, width), jnp.bfloat16),
            jax.ShapeDtypeStruct((length, width), jnp.bfloat16),
        ),
        in_specs=[pl.BlockSpec(memory_space=pltpu.VMEM)] * (len(shards) + len(parts)),
        out_specs=(pl.BlockSpec(memory_space=pltpu.VMEM),) * 2,
        name="project",
        cost_estimate=pl.CostEstimate(
            flops=2 * length * depth * width,
            bytes_accessed=4 * depth * width + 4 * length * width,
            transcendentals=0,
        ),
        compiler_params=pltpu.CompilerParams(vmem_limit_bytes=max(4 << 20, (2 << 20) + 2 * length * depth)),
    )(*shards, *parts)


def product_kernel(dqkv_ref, w_ref, *out_refs, start):
    def multiply(start, out_refs):
        rows = sum(out_ref.shape[0] for out_ref in out_refs)
        whole = dot(dqkv_ref[start : start + rows, :], w_ref[...], NT)
        at = 0
        for out_ref in out_refs:
            out_ref[...] = whole[at : at + out_ref.shape[0]]
            at += out_ref.shape[0]

    for number in range(0, len(out_refs) - 1, 2):
        multiply(start, out_refs[number : number + 2])
        start += 2 * out_refs[number].shape[0]
    multiply(0, out_refs[-1:])


def products(dqkv, w, start, sizes):
    depth, width = w.shape
    return pl.pallas_call(
        functools.partial(product_kernel, start=start),
        out_shape=tuple(jax.ShapeDtypeStruct((size, depth), jnp.float32) for size in sizes),
        name="products",
        cost_estimate=pl.CostEstimate(
            flops=2 * sum(sizes) * depth * width,
            bytes_accessed=2 * depth * width + 6 * sum(sizes) * depth,
            transcendentals=0,
        ),
        compiler_params=pltpu.CompilerParams(vmem_limit_bytes=4 << 20),
    )(dqkv, w)


def join_kernel(own_ref, arrived_ref, out_ref):
    out_ref[...] = (own_ref[...] + arrived_ref[...].astype(jnp.float32)).astype(jnp.bfloat16)


def join(own, arrived):
    return pl.pallas_call(
        join_kernel,
        out_shape=jax.ShapeDtypeStruct(own.shape, jnp.bfloat16),
        out_specs=pl.BlockSpec(memory_space=pltpu.VMEM),
        name="join",
        compiler_params=pltpu.CompilerParams(vmem_limit_bytes=1 << 20),
    )(own, arrived)


def finish_kernel(own_ref, low_ref, high_ref, out_ref):
    half = low_ref.shape[0]
    out_ref[:half, :] = (own_ref[:half, :] + low_ref[...].astype(jnp.float32)).astype(jnp.bfloat16)
    out_ref[half:, :] = (own_ref[half:, :] + high_ref[...].astype(jnp.float32)).astype(jnp.bfloat16)


def finish(own, low, high):
    return pl.pallas_call(
        finish_kernel,
        out_shape=jax.ShapeDtypeStruct(own.shape, jnp.bfloat16),
        name="finish",
        compiler_params=pltpu.CompilerParams(vmem_limit_bytes=2 << 20),
    )(own, low, high)


def attention_kernel(
    packed_ref, early_ref, late_ref, last_ref, w_ref, dout_ref,
    out_ref, dqkv_ref, first_ref, second_ref, place_ref, qkv_ref, kt_ref, vt_ref, *refs,
    heads, all_slots, chunk,
):
    dkv_refs, score_refs, grad_refs, prob_refs, peak_refs = (
        refs[group * heads : (group + 1) * heads] for group in range(5)
    )
    sem = refs[5 * heads]
    length = qkv_ref.shape[0]
    width = heads * HEAD
    tile_count = length // TILE
    scale = HEAD ** (-0.5)
    early = early_ref.shape[0]
    copy = pltpu.make_async_copy(early_ref, qkv_ref.at[pl.ds(0, early)], sem)
    copy.start()
    per_chunk = chunk // TILE
    sp_count = length // chunk
    device = lax.axis_index("sp")
    spot = jnp.where(device % 2 == 0, device // 2, sp_count - 1 - device // 2)
    for number in range(sp_count):
        step = lax.rem(spot - ring_spot(number, sp_count) + sp_count, sp_count)
        for tile in range(per_chunk):
            place_ref[number * per_chunk + tile] = step * per_chunk + tile
    most = packed_ref[heads * tile_count * all_slots]

    def project_late():
        for column in range(0, 3 * width, 2 * HEAD):
            columns = slice(column, column + 2 * HEAD)
            tokens = jnp.concatenate([late_ref[...], last_ref[...]], axis=0)
            qkv_ref[early:, columns] = dot(tokens, w_ref[:, columns], NN).astype(jnp.bfloat16)
            yield True

    def turn_rows(start, stop):
        for head in range(heads):
            at = head * HEAD
            for row in range(start, stop, TILE):
                rows = slice(row, row + TILE)
                kt_ref[head, :, rows] = qkv_ref[rows, width + at : width + at + HEAD].T
                vt_ref[head, :, rows] = qkv_ref[rows, 2 * width + at : 2 * width + at + HEAD].T
                yield True

    def clear():
        for head in range(heads):
            for row in range(0, length, TILE):
                dkv_refs[head][row : row + TILE, :] = jnp.zeros((TILE, 2 * HEAD), jnp.float32)
                yield True

    weave(clear())
    copy.wait()
    weave(project_late(), turn_rows(0, early))
    weave(turn_rows(early, length))

    def tile_rows(tile):
        return pl.ds(pl.multiple_of(tile * TILE, TILE), TILE)

    def spots_of(head, tile, slots):
        base = (head * tile_count + tile) * all_slots
        return base, [tile_rows(place_ref[jnp.maximum(packed_ref[base + s], 0)]) for s in range(slots)]

    def operands(head, tile):
        at = head * HEAD
        query = qkv_ref[tile_rows(place_ref[tile]), at : at + HEAD]
        return query, dout_ref[tile_rows(tile), at : at + HEAD]

    def enter(slots, head, tile):
        at = head * HEAD
        base, spots = spots_of(head, tile, slots)
        query, dout = operands(head, tile)
        peak = None
        empty = jnp.zeros((TILE, HEAD), jnp.bfloat16)
        both = jnp.concatenate([jnp.concatenate([query, empty], axis=1), jnp.concatenate([empty, dout], axis=1)], axis=0)
        for group in groups(slots):
            lhs = [
                jnp.concatenate(
                    [
                        qkv_ref[spots[s], width + at : width + at + HEAD],
                        qkv_ref[spots[s], 2 * width + at : 2 * width + at + HEAD],
                    ],
                    axis=1,
                )
                for s in group
            ]
            parts = dot(jnp.concatenate(lhs, axis=0), both, NT)
            yield True
            for number, s in enumerate(group):
                part = parts[number * TILE : (number + 1) * TILE]
                score = part[:, :TILE]
                if s > 0:
                    score = jnp.where(packed_ref[base + s] >= 0, score, -1e30)
                score_refs[head][s * TILE : (s + 1) * TILE, :] = score
                grad_refs[head][s * TILE : (s + 1) * TILE, :] = part[:, TILE:]
                peak = score if peak is None else jnp.maximum(peak, score)
                yield True
        peak_refs[head][...] = jnp.broadcast_to(jnp.max(peak, axis=0, keepdims=True), (8, TILE))

    def middle(slots, head, tile):
        peak = peak_refs[head][:1, :]
        total = jnp.zeros((1, TILE), jnp.float32)
        delta = jnp.zeros((1, TILE), jnp.float32)
        for s in range(slots):
            part = slice(s * TILE, (s + 1) * TILE)
            grown = jnp.exp2((score_refs[head][part, :] - peak) * (scale * LOG2E))
            score_refs[head][part, :] = grown
            total += jnp.sum(grown, axis=0, keepdims=True)
            delta += jnp.sum(grown * grad_refs[head][part, :], axis=0, keepdims=True)
            yield True
        inverse = 1.0 / total
        delta = delta * inverse
        for s in range(slots):
            part = slice(s * TILE, (s + 1) * TILE)
            prob = score_refs[head][part, :] * inverse
            prob_refs[head][part, TILE:] = prob.astype(jnp.bfloat16)
            prob_refs[head][part, :TILE] = (prob * (grad_refs[head][part, :] - delta) * scale).astype(jnp.bfloat16)
            yield True

    def leave(slots, head, tile):
        at = head * HEAD
        rows = tile_rows(tile)
        held = tile_rows(place_ref[tile])
        _, spots = spots_of(head, tile, slots)
        query, dout = operands(head, tile)
        empty = jnp.zeros((TILE, HEAD), jnp.bfloat16)
        both = jnp.concatenate([jnp.concatenate([query, empty], axis=1), jnp.concatenate([empty, dout], axis=1)], axis=0)
        value_t = jnp.concatenate([vt_ref[head, :, spot] for spot in spots], axis=1)
        out_ref[rows, at : at + HEAD] = dot(value_t, prob_refs[head][: slots * TILE, TILE:], NN).T.astype(jnp.bfloat16)
        yield True
        key_t = jnp.concatenate([kt_ref[head, :, spot] for spot in spots], axis=1)
        dqkv_ref[held, at : at + HEAD] = dot(key_t, prob_refs[head][: slots * TILE, :TILE], NN).T.astype(jnp.bfloat16)
        yield True
        for group in groups(slots):
            parts = dot(prob_refs[head][group[0] * TILE : (group[-1] + 1) * TILE, :], both, NN)
            yield True
            for number, s in enumerate(group):
                dkv_refs[head][spots[s], :] += parts[number * TILE : (number + 1) * TILE]
                yield True

    def before(head, tile, back):
        order = head - back
        return (order % heads, tile + order // heads)

    def turn(slots, tile, first):
        for head in range(heads):
            weave(
                enter(slots, head, tile),
                middle(slots, *before(head, tile, 1)) if not first or head >= 1 else None,
                leave(slots, *before(head, tile, 2)) if not first or head >= 2 else None,
            )

    def run(slots):
        turn(slots, 0, True)

        def step(tile, carry):
            turn(slots, tile, False)
            return carry

        lax.fori_loop(1, tile_count, step, 0)
        last = tile_count - 1
        weave(middle(slots, heads - 1, last), leave(slots, *before(heads, last, 2)))
        weave(leave(slots, heads - 1, last))

    few = all_slots - 1
    if few > 0:
        pl.when(most <= few)(lambda: run(few))
        pl.when(most > few)(lambda: run(all_slots))
    else:
        run(all_slots)
    for head in range(heads):
        at = head * HEAD
        dqkv_ref[:, width + at : width + at + HEAD] = dkv_refs[head][:, :HEAD].astype(jnp.bfloat16)
        dqkv_ref[:, 2 * width + at : 2 * width + at + HEAD] = dkv_refs[head][:, HEAD:].astype(jnp.bfloat16)
    half = chunk // 2
    whole = dot(dqkv_ref[chunk : 2 * chunk, :], w_ref[...], NT).astype(jnp.bfloat16)
    first_ref[...] = whole[:half]
    second_ref[...] = whole[half:]


def attention(early, late, last, w, dout, codes, shape, chunk):
    length = dout.shape[0]
    heads, tile_count, slots = shape
    width = heads * HEAD
    depth = w.shape[0]
    smem = pl.BlockSpec(memory_space=pltpu.SMEM)
    vmem = pl.BlockSpec(memory_space=pltpu.VMEM)
    anywhere = pl.BlockSpec(memory_space=pl.ANY)
    return pl.pallas_call(
        functools.partial(attention_kernel, heads=heads, all_slots=slots, chunk=chunk),
        out_shape=(
            jax.ShapeDtypeStruct((length, width), jnp.bfloat16),
            jax.ShapeDtypeStruct((length, 3 * width), jnp.bfloat16),
            jax.ShapeDtypeStruct((chunk // 2, depth), jnp.bfloat16),
            jax.ShapeDtypeStruct((chunk // 2, depth), jnp.bfloat16),
        ),
        in_specs=[smem, anywhere, vmem, vmem, vmem, vmem],
        out_specs=(vmem, vmem, vmem, vmem),
        scratch_shapes=[
            pltpu.SMEM((tile_count,), jnp.int32),
            pltpu.VMEM((length, 3 * width), jnp.bfloat16),
            pltpu.VMEM((heads, HEAD, length), jnp.bfloat16),
            pltpu.VMEM((heads, HEAD, length), jnp.bfloat16),
        ]
        + [pltpu.VMEM((length, 2 * HEAD), jnp.float32)] * heads
        + [pltpu.VMEM((slots * TILE, TILE), jnp.float32)] * (2 * heads)
        + [pltpu.VMEM((slots * TILE, 2 * TILE), jnp.bfloat16)] * heads
        + [pltpu.VMEM((8, TILE), jnp.float32)] * heads
        + [pltpu.SemaphoreType.DMA],
        name="attention",
        cost_estimate=pl.CostEstimate(
            flops=12 * heads * tile_count * slots * TILE * TILE * HEAD,
            bytes_accessed=16 * length * width,
            transcendentals=heads * tile_count * slots * TILE * TILE,
        ),
        compiler_params=pltpu.CompilerParams(vmem_limit_bytes=14 << 20),
    )(codes, early, late, last, w, dout)


def pack_kernel(code_ref, dout_ref, packed_ref, *, slots):
    rows = code_ref.shape[0] // slots
    most = 1
    for base in range(0, rows * slots, slots):
        packed = [code_ref[base]] + [-1] * (slots - 1)
        count = 1
        for s in range(1, slots):
            code = code_ref[base + s]
            target = jnp.where(code >= 0, count, 0)
            for j in range(1, s + 1):
                packed[j] = jnp.where(target == j, code, packed[j])
            count = count + jnp.where(code >= 0, 1, 0)
        for s in range(slots):
            packed_ref[base + s] = packed[s]
        most = jnp.maximum(most, count)
    packed_ref[rows * slots] = most


def pack(codes, slots, dout):
    smem = pl.BlockSpec(memory_space=pltpu.SMEM)
    return pl.pallas_call(
        functools.partial(pack_kernel, slots=slots),
        out_shape=jax.ShapeDtypeStruct((codes.shape[0] + 1,), jnp.int32),
        in_specs=[smem, pl.BlockSpec(memory_space=pl.ANY)],
        out_specs=smem,
        name="pack",
        compiler_params=pltpu.CompilerParams(vmem_limit_bytes=1 << 20),
    )(codes, dout)


def stagger_kernel(out_ref):
    turns = (lax.axis_index("fsdp") % 2) * PAUSE
    out_ref[0] = lax.fori_loop(0, turns, lambda _, x: (x * 5 + 3) & 1023, turns)


def stagger():
    return pl.pallas_call(
        stagger_kernel,
        out_shape=jax.ShapeDtypeStruct((1,), jnp.int32),
        out_specs=pl.BlockSpec(memory_space=pltpu.SMEM),
        name="stagger",
        compiler_params=pltpu.CompilerParams(has_side_effects=True),
    )()


def ring_spot(device, count):
    return device // 2 if device % 2 == 0 else count - 1 - device // 2


def weight_bits(count):
    return [1 << b for b in range(1, count.bit_length() - 1)]


def gather_weights(w, axis, count):
    def swap(value, bit):
        return lax.ppermute(value, axis, [(i, i ^ bit) for i in range(count)])

    held = {0: w, 1: swap(w, 1)}
    bits = weight_bits(count)
    if len(bits) == 2:
        low, high = bits
        for k in range(2):
            held[low | k] = swap(held[k], low)
            held[high | k] = swap(held[k], high)
        held[low | high] = swap(held[high], low)
        held[low | high | 1] = swap(held[low | 1], high)
    else:
        for bit in bits:
            held.update({k | bit: swap(v, bit) for k, v in list(held.items())})
    return held


def make_shards(fsdp_count, sp_count):
    order = sorted(range(sp_count), key=lambda device: ring_spot(device, sp_count))
    ring = [(order[i], order[(i + 1) % sp_count]) for i in range(sp_count)]

    def layer(tokens_in, w_qkv, grad_attn, kv_tiles, tile_live):
        tokens = tokens_in[0]
        chunk, _ = tokens.shape
        half = chunk // 2
        heads, tile_count, _ = kv_tiles.shape
        length = tile_count * TILE
        width = heads * HEAD
        codes = jnp.where(tile_live > 0, kv_tiles, -1).reshape(-1)
        dout = grad_attn[0].reshape(length, width)
        codes = pack(codes, kv_tiles.shape[2], dout)
        held = gather_weights(w_qkv.reshape(w_qkv.shape[0], -1), "fsdp", fsdp_count)
        halves = [tokens[:half], tokens[half:]]
        parts = [tokens]
        for _ in range(1, sp_count):
            for side in range(2):
                halves[side] = lax.ppermute(halves[side], "sp", ring)
                parts.append(halves[side])
        stagger()
        w, early = project(list(held), list(held.values()), parts[:-2])
        out, dqkv, low, high = attention(
            early, parts[-2], parts[-1], w, dout, codes, kv_tiles.shape, chunk
        )
        sums = products(dqkv, w, 2 * chunk, [half] * (2 * sp_count - 4) + [chunk])
        for step in range(1, sp_count):
            if step > 1:
                low = join(sums[2 * step - 4], low)
            low = lax.ppermute(low, "sp", ring)
            if step > 1:
                high = join(sums[2 * step - 3], high)
            high = lax.ppermute(high, "sp", ring)
        grad_tokens = finish(sums[-1], low, high)
        out = out.reshape(1, length, heads, HEAD)
        return out, grad_tokens[None]

    return layer


def solution(mesh):
    in_specs = (
        P("fsdp", "sp", None),
        P("fsdp", None, "sp", None),
        P("fsdp", None, "sp", None),
        P("sp", None, None),
        P("sp", None, None),
    )
    out_specs = (P("fsdp", None, "sp", None), P("fsdp", "sp", None))
    shards = make_shards(mesh.shape["fsdp"], mesh.shape["sp"])
    return jax.shard_map(shards, mesh=mesh, in_specs=in_specs, out_specs=out_specs, check_vma=False)
```
